32 devices in a mesh: grp: 2 (over y), gz: 4 (over z), gy: 2 (over x), sa: 2 (over core).
Axes of the slice: x: 2, y: 2, z: 4, core: 2. Of those that a mesh axis runs over, the one named last changes fastest.
Arguments:
- field: float32 [8, 32, 16, 128], P('sa', ('grp', 'gz'), 'gy'), parts along dimension 1, may hold values from 0 to 2
- diffusion: float32 [8], P('sa'), may hold values from 0.02 to 0.16
- secrete: float32 [8, 65536], P('sa', ('grp', 'gz', 'gy')), parts along dimension 1, may hold values from 0 to 1
- uptake: float32 [8, 65536], P('sa', ('grp', 'gz', 'gy')), parts along dimension 1, may hold values from 0.05 to 1
- cell_voxel: int32 [65536], P(('grp', 'gz', 'gy')), parts along dimension 0, may hold values from 0 to 4095
- block_dest: int32 [512, 1], P(('grp', 'gz', 'gy')), parts along dimension 0, may hold values from 0 to 3; in each aligned block of 32 rows (0 to 31, 32 to 63, ...) at most 24 rows name the same one
Outputs:
- new_field: float32 [8, 32, 16, 128], P('sa', ('grp', 'gz'), 'gy'), parts along dimension 1
- cell_conc: float32 [8, 65536], P('sa', ('grp', 'gz', 'gy')), parts along dimension 1
The draws below stay inside these ranges and needn't reach their ends.
There are 2 independent parts, one for each index of `grp`. The reference program is written for one: setup_inputs(seed, part) draws one part's arguments, and reference() takes and returns one part's arrays. A program takes and returns all parts, laid end to end along the dimension named above; an argument that names none is the same for every part. Nothing has to cross between parts.
Inputs may be any that keep to these rules, and one draw needn't show every extreme that they name: `block_dest`: among the 32 blocks of one device at most 24 name the same destination, and in every draw some device has exactly 24 blocks naming one destination.
All inputs are finite; a program needn't handle non-finite values.
Results may differ from the reference program's by a relative error of at most 0.00007.
Values sent between devices are 32-bit elements; how exact they have to be, the bound alone decides.
A program may use at most 64 MiB of HBM per device.

```python
import math
import jax
import jax.numpy as jnp
import numpy as np

SUBS = 8
BLOCK_CELLS = 128
BLK_DEV = 32
VZ = 4
VY = 8
NXV = 128
VOX = 4096
NZ = 16
NY = 16
CELLS = 32768
BLOCKS = 256
CAP = 24
N_GZ = 4
N_GY = 2


def plant(drawn, rng, low, largest):
    dims = drawn.shape
    spot = [jax.random.randint(jax.random.fold_in(rng, axis), (), 0, dims[axis]) for axis in range(len(dims))]
    drawn = drawn.at[tuple(spot)].set(low)
    longest = dims.index(max(dims))
    spot[longest] = (spot[longest] + 1) % dims[longest]
    return drawn.at[tuple(spot)].set(largest)


def steps_of(own_key, shape, pieces, smallest, top_value):
    factor_of, own = 1.0, jax.random.fold_in(own_key, 6)
    for axis_at, shards_of in pieces:
        steps = jnp.exp(jax.random.uniform(jax.random.fold_in(own, axis_at), (shards_of,), jnp.float32, smallest / len(pieces), top_value / len(pieces)))
        factor_of = factor_of * jnp.repeat(steps, shape[axis_at] // shards_of).reshape([-1 if axis == axis_at else 1 for axis in range(len(shape))])
    return factor_of


def deal_out(rng, own, number, rows, amount, top, most, lean):
    sequence = jax.random.permutation(rng, amount)
    crowded, ordinary = portions_of(amount, rows * top, most, lean, True), portions_of(amount, rows * top, most, lean, False)
    places = jnp.arange(amount)

    def named(tallies, turn):
        used = int((tallies > 0).sum())
        fixed = max(1, used // 4)
        moved = fixed + (places - fixed + turn * (used - fixed)) % max(1, amount - fixed)
        return jnp.zeros((amount,), jnp.int32).at[sequence[jnp.where(places < fixed, places, moved)]].set(jnp.asarray(tallies, jnp.int32))

    tallies = jnp.where(number % 4 == 0, named(crowded, number // 4), named(ordinary, number - number // 4 - 1))
    mixed = jax.random.permutation(jax.random.fold_in(own, 3), amount)
    giver, sink = mixed[0:amount // 2 * 2:2], mixed[1:amount // 2 * 2:2]
    room = jnp.minimum(tallies[giver] - 1, most - tallies[sink]) // 2
    room = jnp.where((giver == sequence[0]) | (sink == sequence[0]) | (tallies[sink] == 0), 0, jnp.maximum(room, 0))
    moved = jax.random.randint(jax.random.fold_in(own, 4), (amount // 2,), 0, 1 << 20) % (room + 1)
    tallies = tallies.at[giver].add(-moved).at[sink].add(moved)
    members = jnp.searchsorted(jnp.cumsum(tallies), jnp.arange(rows * top), side="right").astype(jnp.int32)
    table = members.reshape(top, rows).T
    table = table[jax.random.permutation(jax.random.fold_in(own, 1), rows)]
    turn = jax.random.randint(jax.random.fold_in(own, 2), (rows, 1), 0, top)
    return jnp.take_along_axis(table, (jnp.arange(top)[None, :] + turn) % top, axis=1)


def portions_of(amount, total, limit, skew, full):
    loads = [(1 << 20) // math.isqrt(grade ** skew) + 1 for grade in range(1, amount + 1)]
    largest = limit if full else min(limit, max(-(-total // amount), total * loads[0] // sum(loads)))
    least = 1 if total - largest >= amount - 1 else 0
    given, rest = [largest] + [least] * (amount - 1), total - largest - least * (amount - 1)
    while rest > 0:
        candidates = [i for i in range(1, amount) if given[i] < largest] or [i for i in range(1, amount) if given[i] < limit]
        pool, left = sum([loads[i] for i in candidates]), rest
        for i in candidates:
            extra = min(limit - given[i], max(1, left * loads[i] // pool), rest)
            given[i] = given[i] + extra
            rest = rest - extra
    return np.array(given)


def setup_inputs(seed: int = 0, part: int = 0) -> dict:
    seeds = jax.random.split(jax.random.key(seed), 7)
    part_splits = jax.random.split(jax.random.fold_in(seeds[6], part), 7)
    field = jnp.clip(2.0 * jax.random.uniform(part_splits[0], (SUBS, NZ, NY, NXV), jnp.float32) ** steps_of(part_splits[0], (SUBS, NZ, NY, NXV), ((0, 2), (1, 4), (2, 2)), -0.2, 0.2), 0.0, 2.0)
    diffusion = jnp.clip(jnp.exp(math.log(0.16) - 2.0794415 * jax.random.uniform(seeds[1], (SUBS,), jnp.float32) ** steps_of(seeds[1], (SUBS,), ((0, 2),), -0.2, 0.2)), 0.02, 0.16)
    secrete = jnp.clip(1.0 * jax.random.uniform(part_splits[2], (SUBS, CELLS), jnp.float32) ** steps_of(part_splits[2], (SUBS, CELLS), ((0, 2), (1, 8)), -0.2, 0.2), 0.0, 1.0)
    uptake = jnp.clip(jnp.exp(math.log(1.0) - 2.9957323 * jax.random.uniform(part_splits[3], (SUBS, CELLS), jnp.float32) ** steps_of(part_splits[3], (SUBS, CELLS), ((0, 2), (1, 8)), -0.2, 0.2)), 0.05, 1.0)
    cell_voxel = plant(jax.random.randint(part_splits[4], (CELLS,), 0, VOX), jax.random.fold_in(part_splits[4], 1), 0, VOX - 1).astype(jnp.int32)
    block_dest_keys = jax.random.split(jax.random.fold_in(part_splits[5], 1), BLOCKS // BLK_DEV)
    block_dest_turns = jax.random.permutation(jax.random.fold_in(part_splits[5], 3), BLOCKS // BLK_DEV)
    block_dest = jax.vmap(lambda own, number: deal_out(jax.random.fold_in(part_splits[5], 2), own, number, BLK_DEV, N_GZ, 1, CAP, 2))(block_dest_keys, block_dest_turns).reshape((BLOCKS, 1))
    return dict(field=field, diffusion=diffusion, secrete=secrete, uptake=uptake, cell_voxel=cell_voxel, block_dest=block_dest)


def neighbours(padded):
    beside_all = padded[:, 2:, 1:-1, 1:-1] + padded[:, :-2, 1:-1, 1:-1]
    beside_all = beside_all + padded[:, 1:-1, 2:, 1:-1] + padded[:, 1:-1, :-2, 1:-1]
    return beside_all + padded[:, 1:-1, 1:-1, 2:] + padded[:, 1:-1, 1:-1, :-2]


def reference(field, diffusion, secrete, uptake, cell_voxel, block_dest):
    padded = jnp.pad(field, ((0, 0), (1, 1), (1, 1), (1, 1)))
    diffused = field + diffusion[:, None, None, None] * (neighbours(padded) - 6.0 * field)
    substrates = field.shape[0]
    cells_total = cell_voxel.shape[0]
    per_device = cells_total // (N_GZ * N_GY)
    cell_index = jnp.arange(cells_total, dtype=jnp.int32)
    home_device = cell_index // per_device
    home_row = home_device % N_GY
    cell_dest = jnp.repeat(block_dest[:, 0], BLOCK_CELLS, total_repeat_length=cells_total)
    voxel_z = cell_voxel // (VY * NXV)
    voxel_y = (cell_voxel // NXV) % VY
    voxel_x = cell_voxel % NXV
    global_z = cell_dest * VZ + voxel_z
    global_y = home_row * VY + voxel_y
    flat_index = ((global_z * NY + global_y) * NXV + voxel_x).astype(jnp.int32)
    total_voxels = NZ * NY * NXV
    source = jnp.zeros((substrates, total_voxels), jnp.float32).at[:, flat_index].add(secrete)
    uptake_sum = jnp.zeros((substrates, total_voxels), jnp.float32).at[:, flat_index].add(uptake)
    updated = (diffused.reshape(substrates, total_voxels) + source) / (1.0 + uptake_sum)
    cell_conc = updated[:, flat_index]
    return updated.reshape(field.shape), cell_conc
```

```python
import functools

import jax
import jax.numpy as jnp
from jax import lax
from jax.experimental import pallas as pl
from jax.experimental.pallas import tpu as pltpu
from jax.sharding import PartitionSpec as P

MESH = pl.DeviceIdType.MESH
F32 = jnp.float32
BF16 = jnp.bfloat16


def split(x):
    high = x.astype(BF16).astype(F32)
    return high, x - high


def kernel(
    n, ny, chunk,
    field, diffusion, secrete, uptake, index,
    updated, conc,
    sec_buf, upt_buf, idx_buf, table, z_low, z_high, y_low, y_high, acc, own_low,
    send_sem, recv_sem, halo_send, halo_recv, tab_send, tab_recv,
):
    z = lax.axis_index("gz")
    y = lax.axis_index("gy")
    subs, planes, rows, lanes = field.shape
    cells = secrete.shape[1]
    width = 2 * lanes
    shift = width.bit_length() - 1
    half = planes * rows // 2
    half_planes = planes // 2
    barrier = pltpu.get_barrier_semaphore()
    sides = (
        (z > 0, {"gz": z - 1}),
        (z < n - 1, {"gz": z + 1}),
        (y > 0, {"gy": y - 1}),
        (y < ny - 1, {"gy": y + 1}),
    )
    for there, device in sides:
        @pl.when(there)
        def _():
            pl.semaphore_signal(barrier, inc=1, device_id=device, device_id_type=MESH)
    pl.semaphore_wait(barrier, sum(jnp.where(there, 1, 0) for there, unused in sides))

    bufs = (idx_buf, sec_buf, upt_buf)
    owns = (index, secrete, uptake)

    def remote(src, dst, send, recv, device):
        return pltpu.make_async_remote_copy(
            src_ref=src, dst_ref=dst, send_sem=send, recv_sem=recv,
            device_id=device, device_id_type=MESH,
        )

    def cell_copy(arr, way, step, slot, src):
        return remote(
            src, bufs[arr].at[slot], send_sem.at[way, step, arr], recv_sem.at[slot, arr],
            sides[way][1],
        )

    def table_copy(way, step, slot, src):
        return remote(
            src, table.at[slot], tab_send.at[way, step], tab_recv.at[slot], sides[way][1]
        )

    halo = (
        remote(field.at[:, 0], z_high, halo_send.at[0], halo_recv.at[0], sides[0][1]),
        remote(field.at[:, planes - 1], z_low, halo_send.at[1], halo_recv.at[1], sides[1][1]),
        remote(field, y_high, halo_send.at[2], halo_recv.at[2], sides[2][1]),
        remote(field, y_low, halo_send.at[3], halo_recv.at[3], sides[3][1]),
    )
    from_side = (1, 0, 3, 2)

    for arr in range(3):
        for way in range(2):
            @pl.when(sides[way][0])
            def _():
                cell_copy(arr, way, 0, z, owns[arr]).start()
    for way in range(4):
        @pl.when(sides[way][0])
        def _():
            halo[way].start()

    acc[...] = jnp.zeros_like(acc)

    def keys(word):
        return lax.shift_right_logical(word, shift), word & (width - 1)

    def deposit(idx, sec, upt, save):
        def step(k, carry):
            at = pl.ds(pl.multiple_of(k * chunk, chunk), chunk)
            key, low = keys(idx[:, at])
            mask = lax.broadcasted_iota(jnp.int32, (half, chunk), 0) == key - half * z
            low_hot = (lax.broadcasted_iota(jnp.int32, (width, chunk), 0) == low).astype(F32)
            low_hot = low_hot.astype(BF16)
            if save:
                own_low[:, at] = low_hot
            parts = split(sec[:, at]) + split(upt[:, at])
            weighted = []
            for part in parts:
                for s in range(subs):
                    row = jnp.broadcast_to(part[s : s + 1], (half, chunk))
                    weighted.append(jnp.where(mask, row, 0.0).astype(BF16))
            weighted = jnp.concatenate(weighted, axis=0)
            acc[...] += lax.dot_general(
                weighted, low_hot, (((1,), (1,)), ((), ())), preferred_element_type=F32
            )
            return carry

        lax.fori_loop(0, cells // chunk, step, 0)

    deposit(index, secrete, uptake, True)

    def gather_step(t, carry):
        slots = (z + t, z - t)
        arrived = (z + t < n, z - t >= 0)
        for arr in range(3):
            for way in range(2):
                slot = slots[way]

                @pl.when(arrived[way])
                def _():
                    remote(
                        bufs[arr].at[slot], bufs[arr].at[slot], send_sem.at[way, t, arr],
                        recv_sem.at[slot, arr], sides[1 - way][1],
                    ).wait_recv()

                    @pl.when(sides[way][0])
                    def _():
                        cell_copy(arr, way, t, slot, bufs[arr].at[slot]).start()
        for way in range(2):
            slot = slots[way]

            @pl.when(arrived[way])
            def _():
                deposit(idx_buf.at[slot], sec_buf.at[slot], upt_buf.at[slot], False)

        return carry

    lax.fori_loop(1, n, gather_step, 0)

    for way in range(4):
        @pl.when(sides[way][0])
        def _():
            halo[from_side[way]].wait_recv()

    lane = lax.broadcasted_iota(jnp.int32, (rows, lanes), 1)
    line = lax.broadcasted_iota(jnp.int32, (rows, lanes), 0)
    has_z = ((z > 0), (z < n - 1))
    has_y = ((y > 0), (y < ny - 1))
    for s in range(subs):
        rate = diffusion[s]
        for p in range(planes):
            here = field[s, p]
            if p > 0:
                below = field[s, p - 1]
            else:
                below = jnp.where(has_z[0], z_low[s], 0.0)
            if p < planes - 1:
                above = field[s, p + 1]
            else:
                above = jnp.where(has_z[1], z_high[s], 0.0)
            edge_low = jnp.where(has_y[0], y_low[s, p], 0.0)
            edge_high = jnp.where(has_y[1], y_high[s, p], 0.0)
            prev = jnp.where(
                line == 0, pltpu.roll(edge_low, 1, 0), pltpu.roll(here, 1, 0)
            )
            following = jnp.where(
                line == rows - 1,
                pltpu.roll(edge_high, rows - 1, 0),
                pltpu.roll(here, rows - 1, 0),
            )
            left = jnp.where(lane == 0, 0.0, pltpu.roll(here, 1, 1))
            right = jnp.where(lane == lanes - 1, 0.0, pltpu.roll(here, lanes - 1, 1))
            total = above + below + following + prev + right + left
            diffused = here + rate * (total - 6.0 * here)
            col = pl.ds((p // half_planes) * lanes, lanes)
            row = (p % half_planes) * rows

            def summed(part):
                first = acc[pl.ds((part * subs + s) * half + row, rows), col]
                return first + acc[pl.ds(((part + 1) * subs + s) * half + row, rows), col]

            updated[s, p] = (diffused + summed(0)) / (1.0 + summed(2))

    for way in range(2):
        @pl.when(sides[way][0])
        def _():
            table_copy(way, 0, z, updated).start()

    def look_up(tab, slot, first):
        left = [tab[:, p].reshape(subs, rows, lanes) for p in range(planes)]
        low_half = jnp.concatenate(left[:half_planes], axis=1)
        high_half = jnp.concatenate(left[half_planes:], axis=1)
        values = jnp.concatenate([low_half, high_half], axis=2).reshape(subs * half, width)
        high_part, low_part = split(values)
        both = jnp.concatenate([high_part, low_part], axis=0).astype(BF16)

        def step(k, carry):
            at = pl.ds(pl.multiple_of(k * chunk, chunk), chunk)
            key, unused = keys(index[:, at])
            mask = lax.broadcasted_iota(jnp.int32, (half, chunk), 0) == key - half * slot
            picked = jnp.dot(both, own_low[:, at], preferred_element_type=F32)
            picked = picked[: subs * half] + picked[subs * half :]
            for s in range(subs):
                part = jnp.where(mask, picked[s * half : (s + 1) * half], 0.0)
                part = jnp.sum(part, axis=0, keepdims=True)
                if first:
                    conc[s : s + 1, at] = part
                else:
                    conc[s : s + 1, at] += part
            return carry

        lax.fori_loop(0, cells // chunk, step, 0)

    look_up(updated, z, True)

    def return_step(t, carry):
        slots = (z + t, z - t)
        arrived = (z + t < n, z - t >= 0)
        for way in range(2):
            slot = slots[way]

            @pl.when(arrived[way])
            def _():
                remote(
                    table.at[slot], table.at[slot], tab_send.at[way, t], tab_recv.at[slot],
                    sides[1 - way][1],
                ).wait_recv()

                @pl.when(sides[way][0])
                def _():
                    table_copy(way, t, slot, table.at[slot]).start()

        for way in range(2):
            slot = slots[way]

            @pl.when(arrived[way])
            def _():
                look_up(table.at[slot], slot, False)

        return carry

    lax.fori_loop(1, n, return_step, 0)

    for way in range(4):
        @pl.when(sides[way][0])
        def _():
            halo[way].wait_send()

    def drain(t, carry):
        slots = (z + t, z - t)
        sent = (z + t < n, z - t >= 0)
        for way in range(2):
            @pl.when(sent[way] & sides[way][0])
            def _():
                for arr in range(3):
                    cell_copy(arr, way, t, slots[way], bufs[arr].at[slots[way]]).wait_send()
                table_copy(way, t, slots[way], table.at[slots[way]]).wait_send()

        return carry

    lax.fori_loop(0, n, drain, 0)


def shards(n, ny, field, diffusion, secrete, uptake, cell_voxel, block_dest):
    subs, planes, rows, lanes = field.shape
    cells = secrete.shape[1]
    blocks = block_dest.shape[0]
    half = planes * rows // 2
    width = 2 * lanes
    assert planes % 2 == 0 and width & (width - 1) == 0
    voxel = cell_voxel.reshape(blocks, cells // blocks)
    line = voxel // lanes
    key = line % half + half * block_dest
    index = (key * width + voxel % lanes + lanes * (line // half)).reshape(1, cells)
    chunk = 512
    dma = pltpu.SemaphoreType.DMA
    vmem = pl.BlockSpec(memory_space=pltpu.VMEM)
    return pl.pallas_call(
        functools.partial(kernel, n, ny, chunk),
        out_shape=(
            jax.ShapeDtypeStruct(field.shape, F32),
            jax.ShapeDtypeStruct(secrete.shape, F32),
        ),
        in_specs=[vmem, pl.BlockSpec(memory_space=pltpu.SMEM), vmem, vmem, vmem],
        out_specs=(vmem, vmem),
        scratch_shapes=[
            pltpu.VMEM((n, subs, cells), F32),
            pltpu.VMEM((n, subs, cells), F32),
            pltpu.VMEM((n, 1, cells), jnp.int32),
            pltpu.VMEM((n,) + field.shape, F32),
            pltpu.VMEM((subs, rows, lanes), F32),
            pltpu.VMEM((subs, rows, lanes), F32),
            pltpu.VMEM(field.shape, F32),
            pltpu.VMEM(field.shape, F32),
            pltpu.VMEM((4 * subs * half, width), F32),
            pltpu.VMEM((width, cells), BF16),
            dma((2, n, 3)),
            dma((n, 3)),
            dma((4,)),
            dma((4,)),
            dma((2, n)),
            dma((n,)),
        ],
        compiler_params=pltpu.CompilerParams(collective_id=0, has_side_effects=True),
    )(field, diffusion, secrete, uptake, index)


def solution(mesh):
    in_specs = (
        P("sa", ("grp", "gz"), "gy", None),
        P("sa"),
        P("sa", ("grp", "gz", "gy")),
        P("sa", ("grp", "gz", "gy")),
        P(("grp", "gz", "gy")),
        P(("grp", "gz", "gy"), None),
    )
    out_specs = (P("sa", ("grp", "gz"), "gy", None), P("sa", ("grp", "gz", "gy")))
    return jax.shard_map(
        functools.partial(shards, mesh.shape["gz"], mesh.shape["gy"]),
        mesh=mesh, in_specs=in_specs, out_specs=out_specs, check_vma=False,
    )
```

```python
import functools

import jax
import jax.numpy as jnp
from jax import lax
from jax.experimental import pallas as pl
from jax.experimental.pallas import tpu as pltpu
from jax.sharding import PartitionSpec as P

MESH = pl.DeviceIdType.MESH
F32 = jnp.float32
BF16 = jnp.bfloat16


def split(x):
    high = x.astype(BF16).astype(F32)
    return high, x - high


def kernel(
    n, ny, chunk, pieces,
    field_in, diffusion, secrete, uptake, voxel_in, targets,
    updated, conc,
    field, voxel, sec_buf, upt_buf, idx_buf, table, z_low, z_high, y_low, y_high, acc, own_low,
    local_sem, send_sem, recv_sem, halo_send, halo_recv, tab_send, tab_recv,
):
    z = lax.axis_index("gz")
    y = lax.axis_index("gy")
    subs, planes, rows, lanes = field.shape
    cells = secrete.shape[1]
    width = 2 * lanes
    shift = width.bit_length() - 1
    half = planes * rows // 2
    half_planes = planes // 2
    blocks = targets.shape[0]
    per_block = cells // blocks
    area = planes * rows
    loads = (
        pltpu.make_async_copy(voxel_in, voxel, local_sem.at[0]),
        pltpu.make_async_copy(secrete, sec_buf.at[z], local_sem.at[1]),
        pltpu.make_async_copy(uptake, upt_buf.at[z], local_sem.at[2]),
        pltpu.make_async_copy(field_in, field, local_sem.at[3]),
    )
    for load in loads:
        load.start()
    barrier = pltpu.get_barrier_semaphore()
    sides = (
        (z > 0, {"gz": z - 1}),
        (z < n - 1, {"gz": z + 1}),
        (y > 0, {"gy": y - 1}),
        (y < ny - 1, {"gy": y + 1}),
    )
    for there, device in sides:
        @pl.when(there)
        def _():
            pl.semaphore_signal(barrier, inc=1, device_id=device, device_id_type=MESH)
    acc[...] = jnp.zeros_like(acc)
    loads[0].wait()
    for b in range(blocks):
        at = pl.ds(b * per_block, per_block)
        own = voxel[:, at]
        line_id = lax.shift_right_logical(own, shift - 1)
        side = jnp.where(line_id >= half, 1, 0)
        key = line_id - half * side + half * targets[b]
        idx_buf[z, :, at] = key * width + (own & (lanes - 1)) + lanes * side
    for load in loads[1:]:
        load.wait()
    pl.semaphore_wait(barrier, sum(jnp.where(there, 1, 0) for there, unused in sides))

    part = cells // 2
    spans = (
        (sec_buf, 0, part), (sec_buf, part, part), (idx_buf, 0, cells),
        (upt_buf, 0, part), (upt_buf, part, part),
    )
    depth = subs * area // pieces

    def cell_ref(arr, slot):
        buf, first, size = spans[arr]
        return buf.at[slot, :, pl.ds(first, size)]

    def table_ref(piece, slot):
        return table.at[slot, pl.ds(piece * depth, depth)]

    def remote(src, dst, send, recv, device):
        return pltpu.make_async_remote_copy(
            src_ref=src, dst_ref=dst, send_sem=send, recv_sem=recv,
            device_id=device, device_id_type=MESH,
        )

    def cell_copy(arr, way, step, slot, side):
        ref = cell_ref(arr, slot)
        return remote(
            ref, ref, send_sem.at[way, step, arr], recv_sem.at[slot, arr], sides[side][1]
        )

    def table_copy(piece, way, step, slot, side):
        ref = table_ref(piece, slot)
        src = updated.at[pl.ds(piece * depth, depth)] if step is None else ref
        return remote(
            src, ref, tab_send.at[way, 0 if step is None else step, piece],
            tab_recv.at[slot, piece], sides[side][1],
        )

    halo = (
        remote(field.at[:, 0], z_high, halo_send.at[0], halo_recv.at[0], sides[0][1]),
        remote(field.at[:, planes - 1], z_low, halo_send.at[1], halo_recv.at[1], sides[1][1]),
        remote(field, y_high, halo_send.at[2], halo_recv.at[2], sides[2][1]),
        remote(field, y_low, halo_send.at[3], halo_recv.at[3], sides[3][1]),
    )
    from_side = (1, 0, 3, 2)

    for arr in range(len(spans)):
        for way in range(2):
            @pl.when(sides[way][0])
            def _():
                cell_copy(arr, way, 0, z, way).start()
    for way in range(4):
        @pl.when(sides[way][0])
        def _():
            halo[way].start()

    def keys(word):
        return lax.shift_right_logical(word, shift), word & (width - 1)

    def deposit(idx, sec, upt, save):
        def step(k, carry):
            at = pl.ds(pl.multiple_of(k * chunk, chunk), chunk)
            key, low = keys(idx[:, at])
            mask = lax.broadcasted_iota(jnp.int32, (half, chunk), 0) == key - half * z
            low_hot = (lax.broadcasted_iota(jnp.int32, (width, chunk), 0) == low).astype(F32)
            low_hot = low_hot.astype(BF16)
            if save:
                own_low[:, at] = low_hot
            parts = split(sec[:, at]) + split(upt[:, at])
            weighted = []
            for part in parts:
                for s in range(subs):
                    row = jnp.broadcast_to(part[s : s + 1], (half, chunk))
                    weighted.append(jnp.where(mask, row, 0.0).astype(BF16))
            weighted = jnp.concatenate(weighted, axis=0)
            acc[...] += lax.dot_general(
                weighted, low_hot, (((1,), (1,)), ((), ())), preferred_element_type=F32
            )
            return carry

        lax.fori_loop(0, cells // chunk, step, 0)

    deposit(idx_buf.at[z], sec_buf.at[z], upt_buf.at[z], True)

    def gather_step(t, carry):
        slots = (z + t, z - t)
        arrived = (z + t < n, z - t >= 0)
        for arr in range(len(spans)):
            for way in range(2):
                slot = slots[way]

                @pl.when(arrived[way])
                def _():
                    cell_copy(arr, way, t, slot, 1 - way).wait_recv()

                    @pl.when(sides[way][0])
                    def _():
                        cell_copy(arr, way, t, slot, way).start()
        for way in range(2):
            slot = slots[way]

            @pl.when(arrived[way])
            def _():
                deposit(idx_buf.at[slot], sec_buf.at[slot], upt_buf.at[slot], False)

        return carry

    lax.fori_loop(1, n, gather_step, 0)

    for way in range(4):
        @pl.when(sides[way][0])
        def _():
            halo[from_side[way]].wait_recv()

    lane = lax.broadcasted_iota(jnp.int32, (rows, lanes), 1)
    line = lax.broadcasted_iota(jnp.int32, (rows, lanes), 0)
    has_z = ((z > 0), (z < n - 1))
    has_y = ((y > 0), (y < ny - 1))
    for s in range(subs):
        rate = diffusion[s]
        for p in range(planes):
            here = field[s, p]
            if p > 0:
                below = field[s, p - 1]
            else:
                below = jnp.where(has_z[0], z_low[s], 0.0)
            if p < planes - 1:
                above = field[s, p + 1]
            else:
                above = jnp.where(has_z[1], z_high[s], 0.0)
            edge_low = jnp.where(has_y[0], y_low[s, p], 0.0)
            edge_high = jnp.where(has_y[1], y_high[s, p], 0.0)
            prev = jnp.where(
                line == 0, pltpu.roll(edge_low, 1, 0), pltpu.roll(here, 1, 0)
            )
            following = jnp.where(
                line == rows - 1,
                pltpu.roll(edge_high, rows - 1, 0),
                pltpu.roll(here, rows - 1, 0),
            )
            left = jnp.where(lane == 0, 0.0, pltpu.roll(here, 1, 1))
            right = jnp.where(lane == lanes - 1, 0.0, pltpu.roll(here, lanes - 1, 1))
            total = above + below + following + prev + right + left
            diffused = here + rate * (total - 6.0 * here)
            col = pl.ds((p // half_planes) * lanes, lanes)
            row = (p % half_planes) * rows

            def summed(part):
                first = acc[pl.ds((part * subs + s) * half + row, rows), col]
                return first + acc[pl.ds(((part + 1) * subs + s) * half + row, rows), col]

            updated[pl.ds((s * planes + p) * rows, rows)] = (diffused + summed(0)) / (1.0 + summed(2))

    for way in range(2):
        @pl.when(sides[way][0])
        def _():
            for piece in range(pieces):
                table_copy(piece, way, None, z, way).start()

    def look_up(tab, slot, first):
        values = tab[...].reshape(subs, 2, half, lanes)
        values = jnp.concatenate([values[:, 0], values[:, 1]], axis=2)
        values = values.reshape(subs * half, width)
        high_part, low_part = split(values)
        both = jnp.concatenate([high_part, low_part], axis=0).astype(BF16)

        def step(k, carry):
            at = pl.ds(pl.multiple_of(k * chunk, chunk), chunk)
            key, unused = keys(idx_buf[z, :, at])
            mask = lax.broadcasted_iota(jnp.int32, (half, chunk), 0) == key - half * slot
            picked = jnp.dot(both, own_low[:, at], preferred_element_type=F32)
            picked = picked[: subs * half] + picked[subs * half :]
            for s in range(subs):
                part = jnp.where(mask, picked[s * half : (s + 1) * half], 0.0)
                part = jnp.sum(part, axis=0, keepdims=True)
                if first:
                    conc[s : s + 1, at] = part
                else:
                    conc[s : s + 1, at] += part
            return carry

        lax.fori_loop(0, cells // chunk, step, 0)

    look_up(updated, z, True)

    def return_step(t, carry):
        slots = (z + t, z - t)
        arrived = (z + t < n, z - t >= 0)
        for piece in range(pieces):
            for way in range(2):
                slot = slots[way]

                @pl.when(arrived[way])
                def _():
                    table_copy(piece, way, t, slot, 1 - way).wait_recv()

                    @pl.when(sides[way][0])
                    def _():
                        table_copy(piece, way, t, slot, way).start()

        for way in range(2):
            slot = slots[way]

            @pl.when(arrived[way])
            def _():
                look_up(table.at[slot], slot, False)

        return carry

    lax.fori_loop(1, n, return_step, 0)

    for way in range(4):
        @pl.when(sides[way][0])
        def _():
            halo[way].wait_send()

    def drain(t, carry):
        slots = (z + t, z - t)
        sent = (z + t < n, z - t >= 0)
        for way in range(2):
            @pl.when(sent[way] & sides[way][0])
            def _():
                for arr in range(len(spans)):
                    cell_copy(arr, way, t, slots[way], way).wait_send()
                for piece in range(pieces):
                    table_copy(piece, way, t, slots[way], way).wait_send()

        return carry

    lax.fori_loop(0, n, drain, 0)


def shards(n, ny, field, diffusion, secrete, uptake, cell_voxel, block_dest):
    subs, planes, rows, lanes = field.shape
    cells = secrete.shape[1]
    blocks = block_dest.shape[0]
    half = planes * rows // 2
    width = 2 * lanes
    assert planes % 2 == 0 and width & (width - 1) == 0
    chunk = 2048
    pieces = 4
    dma = pltpu.SemaphoreType.DMA
    vmem = pl.BlockSpec(memory_space=pltpu.VMEM)
    smem = pl.BlockSpec(memory_space=pltpu.SMEM)
    anywhere = pl.BlockSpec(memory_space=pl.ANY)
    flat = (subs * planes * rows, lanes)
    updated, conc = pl.pallas_call(
        functools.partial(kernel, n, ny, chunk, pieces),
        out_shape=(pltpu.VMEM(flat, F32), pltpu.VMEM(secrete.shape, F32)),
        in_specs=[anywhere, smem, anywhere, anywhere, anywhere, smem],
        out_specs=(vmem, vmem),
        scratch_shapes=[
            pltpu.VMEM(field.shape, F32),
            pltpu.VMEM((1, cells), jnp.int32),
            pltpu.VMEM((n, subs, cells), F32),
            pltpu.VMEM((n, subs, cells), F32),
            pltpu.VMEM((n, 1, cells), jnp.int32),
            pltpu.VMEM((n,) + flat, F32),
            pltpu.VMEM((subs, rows, lanes), F32),
            pltpu.VMEM((subs, rows, lanes), F32),
            pltpu.VMEM(field.shape, F32),
            pltpu.VMEM(field.shape, F32),
            pltpu.VMEM((4 * subs * half, width), F32),
            pltpu.VMEM((width, cells), BF16),
            dma((4,)),
            dma((2, n, 5)),
            dma((n, 5)),
            dma((4,)),
            dma((4,)),
            dma((2, n, pieces)),
            dma((n, pieces)),
        ],
        compiler_params=pltpu.CompilerParams(collective_id=0, has_side_effects=True),
    )(field, diffusion, secrete, uptake, cell_voxel.reshape(1, cells), block_dest.reshape(blocks))
    return updated.reshape(field.shape), conc


def solution(mesh):
    in_specs = (
        P("sa", ("grp", "gz"), "gy", None),
        P("sa"),
        P("sa", ("grp", "gz", "gy")),
        P("sa", ("grp", "gz", "gy")),
        P(("grp", "gz", "gy")),
        P(("grp", "gz", "gy"), None),
    )
    out_specs = (P("sa", ("grp", "gz"), "gy", None), P("sa", ("grp", "gz", "gy")))
    return jax.shard_map(
        functools.partial(shards, mesh.shape["gz"], mesh.shape["gy"]),
        mesh=mesh, in_specs=in_specs, out_specs=out_specs, check_vma=False,
    )
```

```python
import functools

import jax
import jax.numpy as jnp
from jax import lax
from jax.experimental import pallas as pl
from jax.experimental.pallas import tpu as pltpu
from jax.sharding import PartitionSpec as P

MESH = pl.DeviceIdType.MESH
F32 = jnp.float32
BF16 = jnp.bfloat16


def split(x):
    high = x.astype(BF16).astype(F32)
    return high, x - high


def kernel(
    n, ny, chunk, pieces,
    field_in, rates, secrete, uptake, voxel_in, targets_in,
    updated, conc,
    diffusion, targets, field, voxel, sec_buf, upt_buf, idx_buf, table, z_low, z_high, y_low, y_high, acc, own_low,
    local_sem, send_sem, recv_sem, halo_send, halo_recv, tab_send, tab_recv,
):
    z = lax.axis_index("gz")
    y = lax.axis_index("gy")
    subs, planes, rows, lanes = field.shape
    cells = secrete.shape[1]
    width = 2 * lanes
    shift = width.bit_length() - 1
    half = planes * rows // 2
    half_planes = planes // 2
    blocks = targets.shape[0]
    per_block = cells // blocks
    area = planes * rows
    loads = (
        pltpu.make_async_copy(voxel_in, voxel, local_sem.at[0]),
        pltpu.make_async_copy(secrete, sec_buf.at[z], local_sem.at[1]),
        pltpu.make_async_copy(uptake, upt_buf.at[z], local_sem.at[2]),
        pltpu.make_async_copy(field_in, field, local_sem.at[3]),
        pltpu.make_async_copy(rates, diffusion, local_sem.at[4]),
        pltpu.make_async_copy(targets_in, targets, local_sem.at[5]),
    )
    barrier = pltpu.get_barrier_semaphore()
    sides = (
        (z > 0, {"gz": z - 1}),
        (z < n - 1, {"gz": z + 1}),
        (y > 0, {"gy": y - 1}),
        (y < ny - 1, {"gy": y + 1}),
    )
    for there, device in sides:
        @pl.when(there)
        def _():
            pl.semaphore_signal(barrier, inc=1, device_id=device, device_id_type=MESH)
    for load in loads:
        load.start()
    acc[...] = jnp.zeros_like(acc)
    loads[0].wait()
    loads[5].wait()
    for b in range(blocks):
        at = pl.ds(b * per_block, per_block)
        own = voxel[:, at]
        line_id = lax.shift_right_logical(own, shift - 1)
        side = jnp.where(line_id >= half, 1, 0)
        key = line_id - half * side + half * targets[b]
        idx_buf[z, :, at] = key * width + (own & (lanes - 1)) + lanes * side
    for load in loads[1:5]:
        load.wait()
    pl.semaphore_wait(barrier, sum(jnp.where(there, 1, 0) for there, unused in sides))

    part = cells // 2
    spans = (
        (sec_buf, 0, part), (sec_buf, part, part), (idx_buf, 0, cells),
        (upt_buf, 0, part), (upt_buf, part, part),
    )
    depth = subs * area // pieces

    def cell_ref(arr, slot):
        buf, first, size = spans[arr]
        return buf.at[slot, :, pl.ds(first, size)]

    def table_ref(piece, slot):
        return table.at[slot, pl.ds(piece * depth, depth)]

    def remote(src, dst, send, recv, device):
        return pltpu.make_async_remote_copy(
            src_ref=src, dst_ref=dst, send_sem=send, recv_sem=recv,
            device_id=device, device_id_type=MESH,
        )

    def cell_copy(arr, way, step, slot, side):
        ref = cell_ref(arr, slot)
        return remote(
            ref, ref, send_sem.at[way, step, arr], recv_sem.at[slot, arr], sides[side][1]
        )

    def table_copy(piece, way, dist, slot):
        target = z + dist if way else z - dist
        return remote(
            updated.at[pl.ds(piece * depth, depth)], table_ref(piece, slot),
            tab_send.at[way, dist, piece], tab_recv.at[slot, piece], {"gz": target},
        )

    halo = (
        remote(field.at[:, 0], z_high, halo_send.at[0], halo_recv.at[0], sides[0][1]),
        remote(field.at[:, planes - 1], z_low, halo_send.at[1], halo_recv.at[1], sides[1][1]),
        remote(field, y_high, halo_send.at[2], halo_recv.at[2], sides[2][1]),
        remote(field, y_low, halo_send.at[3], halo_recv.at[3], sides[3][1]),
    )
    from_side = (1, 0, 3, 2)

    for arr in range(len(spans)):
        for way in range(2):
            @pl.when(sides[way][0])
            def _():
                cell_copy(arr, way, 0, z, way).start()
    for way in range(4):
        @pl.when(sides[way][0])
        def _():
            halo[way].start()

    def keys(word):
        return lax.shift_right_logical(word, shift), word & (width - 1)

    def deposit(idx, sec, upt, save):
        def step(k, carry):
            at = pl.ds(pl.multiple_of(k * chunk, chunk), chunk)
            key, low = keys(idx[:, at])
            mask = lax.broadcasted_iota(jnp.int32, (half, chunk), 0) == key - half * z
            low_hot = (lax.broadcasted_iota(jnp.int32, (width, chunk), 0) == low).astype(F32)
            low_hot = low_hot.astype(BF16)
            if save:
                own_low[:, at] = low_hot
            parts = split(sec[:, at]) + split(upt[:, at])
            weighted = []
            for part in parts:
                for s in range(subs):
                    row = jnp.broadcast_to(part[s : s + 1], (half, chunk))
                    weighted.append(jnp.where(mask, row, 0.0).astype(BF16))
            weighted = jnp.concatenate(weighted, axis=0)
            acc[...] += lax.dot_general(
                weighted, low_hot, (((1,), (1,)), ((), ())), preferred_element_type=F32
            )
            return carry

        lax.fori_loop(0, cells // chunk, step, 0)

    deposit(idx_buf.at[z], sec_buf.at[z], upt_buf.at[z], True)

    def gather_step(t, carry):
        slots = (z + t, z - t)
        arrived = (z + t < n, z - t >= 0)
        for arr in range(len(spans)):
            for way in range(2):
                slot = slots[way]

                @pl.when(arrived[way])
                def _():
                    cell_copy(arr, way, t, slot, 1 - way).wait_recv()

                    @pl.when(sides[way][0])
                    def _():
                        cell_copy(arr, way, t, slot, way).start()
        for way in range(2):
            slot = slots[way]

            @pl.when(arrived[way])
            def _():
                deposit(idx_buf.at[slot], sec_buf.at[slot], upt_buf.at[slot], False)

        return carry

    lax.fori_loop(1, n, gather_step, 0)

    for way in range(4):
        @pl.when(sides[way][0])
        def _():
            halo[from_side[way]].wait_recv()

    lane = lax.broadcasted_iota(jnp.int32, (rows, lanes), 1)
    line = lax.broadcasted_iota(jnp.int32, (rows, lanes), 0)
    has_z = ((z > 0), (z < n - 1))
    has_y = ((y > 0), (y < ny - 1))
    for s in range(subs):
        rate = diffusion[s]
        for p in range(planes):
            here = field[s, p]
            if p > 0:
                below = field[s, p - 1]
            else:
                below = jnp.where(has_z[0], z_low[s], 0.0)
            if p < planes - 1:
                above = field[s, p + 1]
            else:
                above = jnp.where(has_z[1], z_high[s], 0.0)
            edge_low = jnp.where(has_y[0], y_low[s, p], 0.0)
            edge_high = jnp.where(has_y[1], y_high[s, p], 0.0)
            prev = jnp.where(
                line == 0, pltpu.roll(edge_low, 1, 0), pltpu.roll(here, 1, 0)
            )
            following = jnp.where(
                line == rows - 1,
                pltpu.roll(edge_high, rows - 1, 0),
                pltpu.roll(here, rows - 1, 0),
            )
            left = jnp.where(lane == 0, 0.0, pltpu.roll(here, 1, 1))
            right = jnp.where(lane == lanes - 1, 0.0, pltpu.roll(here, lanes - 1, 1))
            total = above + below + following + prev + right + left
            diffused = here + rate * (total - 6.0 * here)
            col = pl.ds((p // half_planes) * lanes, lanes)
            row = (p % half_planes) * rows

            def summed(part):
                first = acc[pl.ds((part * subs + s) * half + row, rows), col]
                return first + acc[pl.ds(((part + 1) * subs + s) * half + row, rows), col]

            updated[pl.ds((s * planes + p) * rows, rows)] = (diffused + summed(0)) / (1.0 + summed(2))

    def send_table(t, carry):
        dist = n - t
        for way in range(2):
            @pl.when((z + dist < n) if way else (z - dist >= 0))
            def _():
                for piece in range(pieces):
                    table_copy(piece, way, dist, z).start()

        return carry

    lax.fori_loop(1, n, send_table, 0)

    def look_up(tab, slot, first):
        values = tab[...].reshape(subs, 2, half, lanes)
        values = jnp.concatenate([values[:, 0], values[:, 1]], axis=2)
        values = values.reshape(subs * half, width)
        high_part, low_part = split(values)
        both = jnp.concatenate([high_part, low_part], axis=0).astype(BF16)

        def step(k, carry):
            at = pl.ds(pl.multiple_of(k * chunk, chunk), chunk)
            key, unused = keys(idx_buf[z, :, at])
            mask = lax.broadcasted_iota(jnp.int32, (half, chunk), 0) == key - half * slot
            picked = jnp.dot(both, own_low[:, at], preferred_element_type=F32)
            picked = picked[: subs * half] + picked[subs * half :]
            for s in range(subs):
                part = jnp.where(mask, picked[s * half : (s + 1) * half], 0.0)
                part = jnp.sum(part, axis=0, keepdims=True)
                if first:
                    conc[s : s + 1, at] = part
                else:
                    conc[s : s + 1, at] += part
            return carry

        lax.fori_loop(0, cells // chunk, step, 0)

    look_up(updated, z, True)

    def return_step(t, carry):
        slots = (z + t, z - t)
        arrived = (z + t < n, z - t >= 0)
        for way in range(2):
            slot = slots[way]

            @pl.when(arrived[way])
            def _():
                for piece in range(pieces):
                    table_copy(piece, way, t, slot).wait_recv()
                look_up(table.at[slot], slot, False)

        return carry

    lax.fori_loop(1, n, return_step, 0)

    for way in range(4):
        @pl.when(sides[way][0])
        def _():
            halo[way].wait_send()

    def drain(t, carry):
        slots = (z + t, z - t)
        sent = (z + t < n, z - t >= 0)
        for way in range(2):
            @pl.when(sent[way] & sides[way][0])
            def _():
                for arr in range(len(spans)):
                    cell_copy(arr, way, t, slots[way], way).wait_send()

        for way in range(2):
            @pl.when((t > 0) & ((z + t < n) if way else (z - t >= 0)))
            def _():
                for piece in range(pieces):
                    table_copy(piece, way, t, z).wait_send()

        return carry

    lax.fori_loop(0, n, drain, 0)


def shards(n, ny, field, diffusion, secrete, uptake, cell_voxel, block_dest):
    subs, planes, rows, lanes = field.shape
    cells = secrete.shape[1]
    blocks = block_dest.shape[0]
    half = planes * rows // 2
    width = 2 * lanes
    assert planes % 2 == 0 and width & (width - 1) == 0
    chunk = 2048
    pieces = 1
    dma = pltpu.SemaphoreType.DMA
    vmem = pl.BlockSpec(memory_space=pltpu.VMEM)
    anywhere = pl.BlockSpec(memory_space=pl.ANY)
    flat = (subs * planes * rows, lanes)
    updated, conc = pl.pallas_call(
        functools.partial(kernel, n, ny, chunk, pieces),
        out_shape=(pltpu.VMEM(flat, F32), pltpu.VMEM(secrete.shape, F32)),
        in_specs=[anywhere] * 6,
        out_specs=(vmem, vmem),
        scratch_shapes=[
            pltpu.SMEM((subs,), F32),
            pltpu.SMEM((blocks,), jnp.int32),
            pltpu.VMEM(field.shape, F32),
            pltpu.VMEM((1, cells), jnp.int32),
            pltpu.VMEM((n, subs, cells), F32),
            pltpu.VMEM((n, subs, cells), F32),
            pltpu.VMEM((n, 1, cells), jnp.int32),
            pltpu.VMEM((n,) + flat, F32),
            pltpu.VMEM((subs, rows, lanes), F32),
            pltpu.VMEM((subs, rows, lanes), F32),
            pltpu.VMEM(field.shape, F32),
            pltpu.VMEM(field.shape, F32),
            pltpu.VMEM((4 * subs * half, width), F32),
            pltpu.VMEM((width, cells), BF16),
            dma((6,)),
            dma((2, n, 5)),
            dma((n, 5)),
            dma((4,)),
            dma((4,)),
            dma((2, n, pieces)),
            dma((n, pieces)),
        ],
        compiler_params=pltpu.CompilerParams(collective_id=0, has_side_effects=True),
    )(field, diffusion, secrete, uptake, cell_voxel.reshape(1, cells), block_dest.reshape(blocks))
    return updated.reshape(field.shape), conc


def solution(mesh):
    in_specs = (
        P("sa", ("grp", "gz"), "gy", None),
        P("sa"),
        P("sa", ("grp", "gz", "gy")),
        P("sa", ("grp", "gz", "gy")),
        P(("grp", "gz", "gy")),
        P(("grp", "gz", "gy"), None),
    )
    out_specs = (P("sa", ("grp", "gz"), "gy", None), P("sa", ("grp", "gz", "gy")))
    return jax.shard_map(
        functools.partial(shards, mesh.shape["gz"], mesh.shape["gy"]),
        mesh=mesh, in_specs=in_specs, out_specs=out_specs, check_vma=False,
    )
```

```python
import functools

import jax
import jax.numpy as jnp
from jax import lax
from jax.experimental import pallas as pl
from jax.experimental.pallas import tpu as pltpu
from jax.sharding import PartitionSpec as P

MESH = pl.DeviceIdType.MESH
F32 = jnp.float32
BF16 = jnp.bfloat16


def split(x):
    high = x.astype(BF16).astype(F32)
    return high, x - high


def kernel(
    n, ny, chunk, pieces,
    field_in, rates, secrete, uptake, voxel_in, targets_in,
    updated, conc,
    diffusion, targets, field, voxel, sec_buf, upt_buf, idx_buf, table, z_low, z_high, y_low, y_high, acc, own_low,
    local_sem, send_sem, recv_sem, halo_send, halo_recv, tab_send, tab_recv,
):
    z = lax.axis_index("gz")
    y = lax.axis_index("gy")
    subs, planes, rows, lanes = field.shape
    cells = secrete.shape[1]
    width = 2 * lanes
    shift = width.bit_length() - 1
    half = planes * rows // 2
    half_planes = planes // 2
    blocks = targets.shape[0]
    per_block = cells // blocks
    area = planes * rows
    loads = (
        pltpu.make_async_copy(voxel_in, voxel, local_sem.at[0]),
        pltpu.make_async_copy(secrete, sec_buf.at[z], local_sem.at[1]),
        pltpu.make_async_copy(uptake, upt_buf.at[z], local_sem.at[2]),
        pltpu.make_async_copy(field_in, field, local_sem.at[3]),
        pltpu.make_async_copy(rates, diffusion, local_sem.at[4]),
        pltpu.make_async_copy(targets_in, targets, local_sem.at[5]),
    )
    barrier = pltpu.get_barrier_semaphore()
    sides = (
        (z > 0, {"gz": z - 1}),
        (z < n - 1, {"gz": z + 1}),
        (y > 0, {"gy": y - 1}),
        (y < ny - 1, {"gy": y + 1}),
    )
    for there, device in sides:
        @pl.when(there)
        def _():
            pl.semaphore_signal(barrier, inc=1, device_id=device, device_id_type=MESH)
    for load in loads:
        load.start()
    acc[...] = jnp.zeros_like(acc)
    loads[0].wait()
    loads[5].wait()
    for b in range(blocks):
        at = pl.ds(b * per_block, per_block)
        own = voxel[:, at]
        line_id = lax.shift_right_logical(own, shift - 1)
        side = jnp.where(line_id >= half, 1, 0)
        key = line_id - half * side + half * targets[b]
        idx_buf[z, :, at] = key * width + (own & (lanes - 1)) + lanes * side
    for load in loads[1:5]:
        load.wait()
    pl.semaphore_wait(barrier, sum(jnp.where(there, 1, 0) for there, unused in sides))

    part = cells // 2
    spans = (
        (sec_buf, 0, part), (idx_buf, 0, cells), (upt_buf, 0, part),
        (sec_buf, part, part), (upt_buf, part, part),
    )
    depth = subs * area // pieces

    def cell_ref(arr, slot):
        buf, first, size = spans[arr]
        return buf.at[slot, :, pl.ds(first, size)]

    def table_ref(piece, slot):
        return table.at[slot, pl.ds(piece * depth, depth)]

    def remote(src, dst, send, recv, device):
        return pltpu.make_async_remote_copy(
            src_ref=src, dst_ref=dst, send_sem=send, recv_sem=recv,
            device_id=device, device_id_type=MESH,
        )

    def cell_copy(arr, way, step, slot, side):
        ref = cell_ref(arr, slot)
        return remote(
            ref, ref, send_sem.at[way, step, arr], recv_sem.at[slot, arr], sides[side][1]
        )

    def table_copy(piece, way, dist, slot):
        target = z + dist if way else z - dist
        return remote(
            updated.at[pl.ds(piece * depth, depth)], table_ref(piece, slot),
            tab_send.at[way, dist, piece], tab_recv.at[slot, piece], {"gz": target},
        )

    halo = (
        remote(field.at[:, 0], z_high, halo_send.at[0], halo_recv.at[0], sides[0][1]),
        remote(field.at[:, planes - 1], z_low, halo_send.at[1], halo_recv.at[1], sides[1][1]),
        remote(field, y_high, halo_send.at[2], halo_recv.at[2], sides[2][1]),
        remote(field, y_low, halo_send.at[3], halo_recv.at[3], sides[3][1]),
    )
    from_side = (1, 0, 3, 2)

    for arr in range(len(spans)):
        for way in range(2):
            @pl.when(sides[way][0])
            def _():
                cell_copy(arr, way, 0, z, way).start()
    for way in range(4):
        @pl.when(sides[way][0])
        def _():
            halo[way].start()

    def keys(word):
        return lax.shift_right_logical(word, shift), word & (width - 1)

    def deposit(idx, sec, upt, save, first=0, last=cells):
        def step(k, carry):
            at = pl.ds(pl.multiple_of(k * chunk, chunk), chunk)
            key, low = keys(idx[:, at])
            mask = lax.broadcasted_iota(jnp.int32, (half, chunk), 0) == key - half * z
            low_hot = (lax.broadcasted_iota(jnp.int32, (width, chunk), 0) == low).astype(F32)
            low_hot = low_hot.astype(BF16)
            if save:
                own_low[:, at] = low_hot
            parts = split(sec[:, at]) + split(upt[:, at])
            weighted = []
            for part in parts:
                for s in range(subs):
                    row = jnp.broadcast_to(part[s : s + 1], (half, chunk))
                    weighted.append(jnp.where(mask, row, 0.0).astype(BF16))
            weighted = jnp.concatenate(weighted, axis=0)
            acc[...] += lax.dot_general(
                weighted, low_hot, (((1,), (1,)), ((), ())), preferred_element_type=F32
            )
            return carry

        lax.fori_loop(first // chunk, last // chunk, step, 0)

    deposit(idx_buf.at[z], sec_buf.at[z], upt_buf.at[z], True)

    def gather_step(t, carry):
        slots = (z + t, z - t)
        arrived = (z + t < n, z - t >= 0)
        for arr in range(len(spans)):
            for way in range(2):
                slot = slots[way]

                @pl.when(arrived[way])
                def _():
                    cell_copy(arr, way, t, slot, 1 - way).wait_recv()

                    @pl.when(sides[way][0])
                    def _():
                        cell_copy(arr, way, t, slot, way).start()

            if arr not in (2, 4):
                continue
            first = 0 if arr == 2 else part
            for way in range(2):
                slot = slots[way]

                @pl.when(arrived[way])
                def _():
                    deposit(
                        idx_buf.at[slot], sec_buf.at[slot], upt_buf.at[slot], False,
                        first, first + part,
                    )

        return carry

    lax.fori_loop(1, n, gather_step, 0)

    for way in range(4):
        @pl.when(sides[way][0])
        def _():
            halo[from_side[way]].wait_recv()

    lane = lax.broadcasted_iota(jnp.int32, (rows, lanes), 1)
    line = lax.broadcasted_iota(jnp.int32, (rows, lanes), 0)
    has_z = ((z > 0), (z < n - 1))
    has_y = ((y > 0), (y < ny - 1))
    for s in range(subs):
        rate = diffusion[s]
        for p in range(planes):
            here = field[s, p]
            if p > 0:
                below = field[s, p - 1]
            else:
                below = jnp.where(has_z[0], z_low[s], 0.0)
            if p < planes - 1:
                above = field[s, p + 1]
            else:
                above = jnp.where(has_z[1], z_high[s], 0.0)
            edge_low = jnp.where(has_y[0], y_low[s, p], 0.0)
            edge_high = jnp.where(has_y[1], y_high[s, p], 0.0)
            prev = jnp.where(
                line == 0, pltpu.roll(edge_low, 1, 0), pltpu.roll(here, 1, 0)
            )
            following = jnp.where(
                line == rows - 1,
                pltpu.roll(edge_high, rows - 1, 0),
                pltpu.roll(here, rows - 1, 0),
            )
            left = jnp.where(lane == 0, 0.0, pltpu.roll(here, 1, 1))
            right = jnp.where(lane == lanes - 1, 0.0, pltpu.roll(here, lanes - 1, 1))
            total = above + below + following + prev + right + left
            diffused = here + rate * (total - 6.0 * here)
            col = pl.ds((p // half_planes) * lanes, lanes)
            row = (p % half_planes) * rows

            def summed(part):
                first = acc[pl.ds((part * subs + s) * half + row, rows), col]
                return first + acc[pl.ds(((part + 1) * subs + s) * half + row, rows), col]

            updated[pl.ds((s * planes + p) * rows, rows)] = (diffused + summed(0)) / (1.0 + summed(2))

    def send_table(t, carry):
        dist = n - t
        for way in range(2):
            @pl.when((z + dist < n) if way else (z - dist >= 0))
            def _():
                for piece in range(pieces):
                    table_copy(piece, way, dist, z).start()

        return carry

    lax.fori_loop(1, n, send_table, 0)

    def look_up(tab, slot, first):
        values = tab[...].reshape(subs, 2, half, lanes)
        values = jnp.concatenate([values[:, 0], values[:, 1]], axis=2)
        values = values.reshape(subs * half, width)
        high_part, low_part = split(values)
        both = jnp.concatenate([high_part, low_part], axis=0).astype(BF16)

        def step(k, carry):
            at = pl.ds(pl.multiple_of(k * chunk, chunk), chunk)
            key, unused = keys(idx_buf[z, :, at])
            mask = lax.broadcasted_iota(jnp.int32, (half, chunk), 0) == key - half * slot
            picked = jnp.dot(both, own_low[:, at], preferred_element_type=F32)
            picked = picked[: subs * half] + picked[subs * half :]
            for s in range(subs):
                part = jnp.where(mask, picked[s * half : (s + 1) * half], 0.0)
                part = jnp.sum(part, axis=0, keepdims=True)
                if first:
                    conc[s : s + 1, at] = part
                else:
                    conc[s : s + 1, at] += part
            return carry

        lax.fori_loop(0, cells // chunk, step, 0)

    look_up(updated, z, True)

    toward = jnp.where(2 * z < n, 1, -1)
    for turn in (1, -1):
        def return_step(t, carry):
            slot = z + turn * toward * t

            @pl.when((slot >= 0) & (slot < n))
            def _():
                for piece in range(pieces):
                    remote(
                        table_ref(piece, slot), table_ref(piece, slot), tab_send.at[0, t, piece],
                        tab_recv.at[slot, piece], {"gz": slot},
                    ).wait_recv()
                look_up(table.at[slot], slot, False)

            return carry

        lax.fori_loop(1, n, return_step, 0)

    for way in range(4):
        @pl.when(sides[way][0])
        def _():
            halo[way].wait_send()

    def drain(t, carry):
        slots = (z + t, z - t)
        sent = (z + t < n, z - t >= 0)
        for way in range(2):
            @pl.when(sent[way] & sides[way][0])
            def _():
                for arr in range(len(spans)):
                    cell_copy(arr, way, t, slots[way], way).wait_send()

        for way in range(2):
            @pl.when((t > 0) & ((z + t < n) if way else (z - t >= 0)))
            def _():
                for piece in range(pieces):
                    table_copy(piece, way, t, z).wait_send()

        return carry

    lax.fori_loop(0, n, drain, 0)


def shards(n, ny, field, diffusion, secrete, uptake, cell_voxel, block_dest):
    subs, planes, rows, lanes = field.shape
    cells = secrete.shape[1]
    blocks = block_dest.shape[0]
    half = planes * rows // 2
    width = 2 * lanes
    assert planes % 2 == 0 and width & (width - 1) == 0
    chunk = 2048
    pieces = 1
    dma = pltpu.SemaphoreType.DMA
    vmem = pl.BlockSpec(memory_space=pltpu.VMEM)
    anywhere = pl.BlockSpec(memory_space=pl.ANY)
    flat = (subs * planes * rows, lanes)
    updated, conc = pl.pallas_call(
        functools.partial(kernel, n, ny, chunk, pieces),
        out_shape=(pltpu.VMEM(flat, F32), pltpu.VMEM(secrete.shape, F32)),
        in_specs=[anywhere] * 6,
        out_specs=(vmem, vmem),
        scratch_shapes=[
            pltpu.SMEM((subs,), F32),
            pltpu.SMEM((blocks,), jnp.int32),
            pltpu.VMEM(field.shape, F32),
            pltpu.VMEM((1, cells), jnp.int32),
            pltpu.VMEM((n, subs, cells), F32),
            pltpu.VMEM((n, subs, cells), F32),
            pltpu.VMEM((n, 1, cells), jnp.int32),
            pltpu.VMEM((n,) + flat, F32),
            pltpu.VMEM((subs, rows, lanes), F32),
            pltpu.VMEM((subs, rows, lanes), F32),
            pltpu.VMEM(field.shape, F32),
            pltpu.VMEM(field.shape, F32),
            pltpu.VMEM((4 * subs * half, width), F32),
            pltpu.VMEM((width, cells), BF16),
            dma((6,)),
            dma((2, n, 5)),
            dma((n, 5)),
            dma((4,)),
            dma((4,)),
            dma((2, n, pieces)),
            dma((n, pieces)),
        ],
        compiler_params=pltpu.CompilerParams(collective_id=0, has_side_effects=True),
    )(field, diffusion, secrete, uptake, cell_voxel.reshape(1, cells), block_dest.reshape(blocks))
    return updated.reshape(field.shape), conc


def solution(mesh):
    in_specs = (
        P("sa", ("grp", "gz"), "gy", None),
        P("sa"),
        P("sa", ("grp", "gz", "gy")),
        P("sa", ("grp", "gz", "gy")),
        P(("grp", "gz", "gy")),
        P(("grp", "gz", "gy"), None),
    )
    out_specs = (P("sa", ("grp", "gz"), "gy", None), P("sa", ("grp", "gz", "gy")))
    return jax.shard_map(
        functools.partial(shards, mesh.shape["gz"], mesh.shape["gy"]),
        mesh=mesh, in_specs=in_specs, out_specs=out_specs, check_vma=False,
    )
```

```python
import functools

import jax
import jax.numpy as jnp
from jax import lax
from jax.experimental import pallas as pl
from jax.experimental.pallas import tpu as pltpu
from jax.sharding import PartitionSpec as P

MESH = pl.DeviceIdType.MESH
F32 = jnp.float32
BF16 = jnp.bfloat16


def split(x):
    high = x.astype(BF16).astype(F32)
    return high, x - high


def kernel(
    n, ny, chunk, pieces,
    field_in, rates, secrete, uptake, voxel_in, targets_in,
    updated, conc,
    diffusion, targets, field, voxel, sec_buf, upt_buf, idx_buf, table, z_low, z_high, y_low, y_high, acc, own_low,
    local_sem, send_sem, recv_sem, halo_send, halo_recv, tab_send, tab_recv,
):
    z = lax.axis_index("gz")
    y = lax.axis_index("gy")
    subs, planes, rows, lanes = field.shape
    cells = secrete.shape[1]
    width = 2 * lanes
    shift = width.bit_length() - 1
    half = planes * rows // 2
    half_planes = planes // 2
    blocks = targets.shape[0]
    per_block = cells // blocks
    area = planes * rows
    loads = (
        pltpu.make_async_copy(voxel_in, voxel, local_sem.at[0]),
        pltpu.make_async_copy(secrete, sec_buf.at[z], local_sem.at[1]),
        pltpu.make_async_copy(uptake, upt_buf.at[z], local_sem.at[2]),
        pltpu.make_async_copy(field_in, field, local_sem.at[3]),
        pltpu.make_async_copy(rates, diffusion, local_sem.at[4]),
        pltpu.make_async_copy(targets_in, targets, local_sem.at[5]),
    )
    barrier = pltpu.get_barrier_semaphore()
    sides = (
        (z > 0, {"gz": z - 1}),
        (z < n - 1, {"gz": z + 1}),
        (y > 0, {"gy": y - 1}),
        (y < ny - 1, {"gy": y + 1}),
    )
    for there, device in sides:
        @pl.when(there)
        def _():
            pl.semaphore_signal(barrier, inc=1, device_id=device, device_id_type=MESH)
    for load in loads:
        load.start()
    acc[...] = jnp.zeros_like(acc)
    loads[0].wait()
    loads[5].wait()
    for b in range(blocks):
        at = pl.ds(b * per_block, per_block)
        own = voxel[:, at]
        line_id = lax.shift_right_logical(own, shift - 1)
        side = jnp.where(line_id >= half, 1, 0)
        key = line_id - half * side + half * targets[b]
        idx_buf[z, :, at] = key * width + (own & (lanes - 1)) + lanes * side
    for load in loads[1:5]:
        load.wait()
    pl.semaphore_wait(barrier, sum(jnp.where(there, 1, 0) for there, unused in sides))

    part = cells // 2
    spans = (
        (sec_buf, 0, part), (idx_buf, 0, part), (upt_buf, 0, part),
        (idx_buf, part, part), (sec_buf, part, part), (upt_buf, part, part),
    )
    depth = subs * area // pieces

    def cell_ref(arr, slot):
        buf, first, size = spans[arr]
        return buf.at[slot, :, pl.ds(first, size)]

    def table_ref(piece, slot):
        return table.at[slot, pl.ds(piece * depth, depth)]

    def remote(src, dst, send, recv, device):
        return pltpu.make_async_remote_copy(
            src_ref=src, dst_ref=dst, send_sem=send, recv_sem=recv,
            device_id=device, device_id_type=MESH,
        )

    def cell_copy(arr, way, step, slot, side):
        ref = cell_ref(arr, slot)
        return remote(
            ref, ref, send_sem.at[way, step, arr], recv_sem.at[slot, arr], sides[side][1]
        )

    def table_copy(piece, way, dist, slot):
        target = z + dist if way else z - dist
        return remote(
            updated.at[pl.ds(piece * depth, depth)], table_ref(piece, slot),
            tab_send.at[way, dist, piece], tab_recv.at[slot, piece], {"gz": target},
        )

    halo = (
        remote(field.at[:, 0], z_high, halo_send.at[0], halo_recv.at[0], sides[0][1]),
        remote(field.at[:, planes - 1], z_low, halo_send.at[1], halo_recv.at[1], sides[1][1]),
        remote(field, y_high, halo_send.at[2], halo_recv.at[2], sides[2][1]),
        remote(field, y_low, halo_send.at[3], halo_recv.at[3], sides[3][1]),
    )
    from_side = (1, 0, 3, 2)

    for arr in range(len(spans)):
        for way in range(2):
            @pl.when(sides[way][0])
            def _():
                cell_copy(arr, way, 0, z, way).start()
    for way in range(4):
        @pl.when(sides[way][0])
        def _():
            halo[way].start()

    def keys(word):
        return lax.shift_right_logical(word, shift), word & (width - 1)

    def deposit(idx, sec, upt, save, first=0, last=cells):
        def step(k, carry):
            at = pl.ds(pl.multiple_of(k * chunk, chunk), chunk)
            key, low = keys(idx[:, at])
            mask = lax.broadcasted_iota(jnp.int32, (half, chunk), 0) == key - half * z
            low_hot = (lax.broadcasted_iota(jnp.int32, (width, chunk), 0) == low).astype(F32)
            low_hot = low_hot.astype(BF16)
            if save:
                own_low[:, at] = low_hot
            parts = split(sec[:, at]) + split(upt[:, at])
            weighted = []
            for part in parts:
                for s in range(subs):
                    row = jnp.broadcast_to(part[s : s + 1], (half, chunk))
                    weighted.append(jnp.where(mask, row, 0.0).astype(BF16))
            weighted = jnp.concatenate(weighted, axis=0)
            acc[...] += lax.dot_general(
                weighted, low_hot, (((1,), (1,)), ((), ())), preferred_element_type=F32
            )
            return carry

        lax.fori_loop(first // chunk, last // chunk, step, 0)

    deposit(idx_buf.at[z], sec_buf.at[z], upt_buf.at[z], True)

    def gather_step(t, carry):
        slots = (z + t, z - t)
        arrived = (z + t < n, z - t >= 0)
        for arr in range(len(spans)):
            for way in range(2):
                slot = slots[way]

                @pl.when(arrived[way])
                def _():
                    cell_copy(arr, way, t, slot, 1 - way).wait_recv()

                    @pl.when(sides[way][0])
                    def _():
                        cell_copy(arr, way, t, slot, way).start()

            if arr not in (2, 5):
                continue
            first = 0 if arr == 2 else part
            for way in range(2):
                slot = slots[way]

                @pl.when(arrived[way])
                def _():
                    deposit(
                        idx_buf.at[slot], sec_buf.at[slot], upt_buf.at[slot], False,
                        first, first + part,
                    )

        return carry

    lax.fori_loop(1, n, gather_step, 0)

    for way in range(4):
        @pl.when(sides[way][0])
        def _():
            halo[from_side[way]].wait_recv()

    lane = lax.broadcasted_iota(jnp.int32, (rows, lanes), 1)
    line = lax.broadcasted_iota(jnp.int32, (rows, lanes), 0)
    has_z = ((z > 0), (z < n - 1))
    has_y = ((y > 0), (y < ny - 1))
    for s in range(subs):
        rate = diffusion[s]
        for p in range(planes):
            here = field[s, p]
            if p > 0:
                below = field[s, p - 1]
            else:
                below = jnp.where(has_z[0], z_low[s], 0.0)
            if p < planes - 1:
                above = field[s, p + 1]
            else:
                above = jnp.where(has_z[1], z_high[s], 0.0)
            edge_low = jnp.where(has_y[0], y_low[s, p], 0.0)
            edge_high = jnp.where(has_y[1], y_high[s, p], 0.0)
            prev = jnp.where(
                line == 0, pltpu.roll(edge_low, 1, 0), pltpu.roll(here, 1, 0)
            )
            following = jnp.where(
                line == rows - 1,
                pltpu.roll(edge_high, rows - 1, 0),
                pltpu.roll(here, rows - 1, 0),
            )
            left = jnp.where(lane == 0, 0.0, pltpu.roll(here, 1, 1))
            right = jnp.where(lane == lanes - 1, 0.0, pltpu.roll(here, lanes - 1, 1))
            total = above + below + following + prev + right + left
            diffused = here + rate * (total - 6.0 * here)
            col = pl.ds((p // half_planes) * lanes, lanes)
            row = (p % half_planes) * rows

            def summed(part):
                first = acc[pl.ds((part * subs + s) * half + row, rows), col]
                return first + acc[pl.ds(((part + 1) * subs + s) * half + row, rows), col]

            updated[pl.ds((s * planes + p) * rows, rows)] = (diffused + summed(0)) / (1.0 + summed(2))

    def send_table(t, carry):
        dist = n - t
        for way in range(2):
            @pl.when((z + dist < n) if way else (z - dist >= 0))
            def _():
                for piece in range(pieces):
                    table_copy(piece, way, dist, z).start()

        return carry

    lax.fori_loop(1, n, send_table, 0)

    def look_up(tab, slot, first):
        values = tab[...].reshape(subs, 2, half, lanes)
        values = jnp.concatenate([values[:, 0], values[:, 1]], axis=2)
        values = values.reshape(subs * half, width)
        high_part, low_part = split(values)
        both = jnp.concatenate([high_part, low_part], axis=0).astype(BF16)

        def step(k, carry):
            at = pl.ds(pl.multiple_of(k * chunk, chunk), chunk)
            key, unused = keys(idx_buf[z, :, at])
            mask = lax.broadcasted_iota(jnp.int32, (half, chunk), 0) == key - half * slot
            picked = jnp.dot(both, own_low[:, at], preferred_element_type=F32)
            picked = picked[: subs * half] + picked[subs * half :]
            for s in range(subs):
                part = jnp.where(mask, picked[s * half : (s + 1) * half], 0.0)
                part = jnp.sum(part, axis=0, keepdims=True)
                if first:
                    conc[s : s + 1, at] = part
                else:
                    conc[s : s + 1, at] += part
            return carry

        lax.fori_loop(0, cells // chunk, step, 0)

    look_up(updated, z, True)

    toward = jnp.where(2 * z < n, 1, -1)
    for turn in (1, -1):
        def return_step(t, carry):
            slot = z + turn * toward * t

            @pl.when((slot >= 0) & (slot < n))
            def _():
                for piece in range(pieces):
                    remote(
                        table_ref(piece, slot), table_ref(piece, slot), tab_send.at[0, t, piece],
                        tab_recv.at[slot, piece], {"gz": slot},
                    ).wait_recv()
                look_up(table.at[slot], slot, False)

            return carry

        lax.fori_loop(1, n, return_step, 0)

    for way in range(4):
        @pl.when(sides[way][0])
        def _():
            halo[way].wait_send()

    def drain(t, carry):
        slots = (z + t, z - t)
        sent = (z + t < n, z - t >= 0)
        for way in range(2):
            @pl.when(sent[way] & sides[way][0])
            def _():
                for arr in range(len(spans)):
                    cell_copy(arr, way, t, slots[way], way).wait_send()

        for way in range(2):
            @pl.when((t > 0) & ((z + t < n) if way else (z - t >= 0)))
            def _():
                for piece in range(pieces):
                    table_copy(piece, way, t, z).wait_send()

        return carry

    lax.fori_loop(0, n, drain, 0)


def shards(n, ny, field, diffusion, secrete, uptake, cell_voxel, block_dest):
    subs, planes, rows, lanes = field.shape
    cells = secrete.shape[1]
    blocks = block_dest.shape[0]
    half = planes * rows // 2
    width = 2 * lanes
    assert planes % 2 == 0 and width & (width - 1) == 0
    chunk = 2048
    pieces = 1
    dma = pltpu.SemaphoreType.DMA
    vmem = pl.BlockSpec(memory_space=pltpu.VMEM)
    anywhere = pl.BlockSpec(memory_space=pl.ANY)
    flat = (subs * planes * rows, lanes)
    updated, conc = pl.pallas_call(
        functools.partial(kernel, n, ny, chunk, pieces),
        out_shape=(pltpu.VMEM(flat, F32), pltpu.VMEM(secrete.shape, F32)),
        in_specs=[anywhere] * 6,
        out_specs=(vmem, vmem),
        scratch_shapes=[
            pltpu.SMEM((subs,), F32),
            pltpu.SMEM((blocks,), jnp.int32),
            pltpu.VMEM(field.shape, F32),
            pltpu.VMEM((1, cells), jnp.int32),
            pltpu.VMEM((n, subs, cells), F32),
            pltpu.VMEM((n, subs, cells), F32),
            pltpu.VMEM((n, 1, cells), jnp.int32),
            pltpu.VMEM((n,) + flat, F32),
            pltpu.VMEM((subs, rows, lanes), F32),
            pltpu.VMEM((subs, rows, lanes), F32),
            pltpu.VMEM(field.shape, F32),
            pltpu.VMEM(field.shape, F32),
            pltpu.VMEM((4 * subs * half, width), F32),
            pltpu.VMEM((width, cells), BF16),
            dma((6,)),
            dma((2, n, 6)),
            dma((n, 6)),
            dma((4,)),
            dma((4,)),
            dma((2, n, pieces)),
            dma((n, pieces)),
        ],
        compiler_params=pltpu.CompilerParams(collective_id=0, has_side_effects=True),
    )(field, diffusion, secrete, uptake, cell_voxel.reshape(1, cells), block_dest.reshape(blocks))
    return updated.reshape(field.shape), conc


def solution(mesh):
    in_specs = (
        P("sa", ("grp", "gz"), "gy", None),
        P("sa"),
        P("sa", ("grp", "gz", "gy")),
        P("sa", ("grp", "gz", "gy")),
        P(("grp", "gz", "gy")),
        P(("grp", "gz", "gy"), None),
    )
    out_specs = (P("sa", ("grp", "gz"), "gy", None), P("sa", ("grp", "gz", "gy")))
    return jax.shard_map(
        functools.partial(shards, mesh.shape["gz"], mesh.shape["gy"]),
        mesh=mesh, in_specs=in_specs, out_specs=out_specs, check_vma=False,
    )
```
